1024 devices in a mesh: leaf: 64 (over x, z), sub: 16 (over y, core).
Axes of the slice: x: 8, y: 8, z: 8, core: 2. Of those that a mesh axis runs over, the one named last changes fastest.
Arguments:
- coarse_scaling: float32 [512, 131072], P(None, ('leaf', 'sub')), may hold values from -6 to 6
- details: bfloat16 [2, 3584, 131072], P(None, None, ('leaf', 'sub')), may hold values from -6 to 6
- two_scale: float32 [16, 16], replicated, may hold values from -1 to 1, as said below
- parent_link: int32 [2, 131072], P(None, ('leaf', 'sub')), may hold values from -1 to 1048575, as said below
Outputs:
- leaf_scaling: float32 [512, 131072], P(None, ('leaf', 'sub'))
The draws below stay inside these ranges and needn't reach their ends.
Inputs may be any that keep to these rules, and one draw needn't show every extreme that they name: `parent_link`: slots are numbered leaf-major over the devices, 128 to a device. A box that has children has all eight, in eight consecutive slots in octant order. A box's parent stands on the same device, or in the last 4 slots of the previous device; each of those 4 boxes (except on the last device) has its eight children in the last 32 slots of the next device, and none on its own. Parents are live boxes (the level above has a link that is not -1, or is level 0). The last 4 slots of every device are live at every level. `two_scale`: an orthogonal matrix.
All inputs are finite; a program needn't handle non-finite values.
Results may differ from the reference program's by a relative error of at most 0.0003.
Values sent between devices are 32-bit elements; how exact they have to be, the bound alone decides.
A program may use at most 128 MiB of HBM per device.

```python
import jax
import jax.numpy as jnp
from jax import lax

K = 8
SLOTS = 128
TAIL = 4
LEVELS = 2
BOXES = 131072


def draw_two_scale(key, part):
    drawn = jax.random.normal(key, (2 * K, 2 * K), jnp.float32)
    columns = []
    for position in range(2 * K):
        vector = drawn[:, position]
        for earlier in columns:
            vector = vector - jnp.dot(earlier, vector) * earlier
        vector = vector / jnp.sqrt(jnp.sum(vector * vector))
        columns.append(vector)
    return jnp.stack(columns, 1)


def draw_parent_link(key, part):
    device_count = BOXES // SLOTS
    boundary = SLOTS - TAIL
    received_start = SLOTS - 8 * TAIL
    most_refined = (SLOTS - 8 * TAIL) // 8
    least_refined = max(1, most_refined // 2)
    picked_count = most_refined + TAIL
    slot_index = jnp.arange(SLOTS, dtype=jnp.int32)[None, :]
    device_ids = jnp.arange(device_count, dtype=jnp.int32)[:, None]
    is_first = device_ids == 0
    prev_live = jnp.ones((device_count, SLOTS), dtype=bool)
    levels_out = []
    for level_index in range(LEVELS):
        key_level = jax.random.fold_in(key, 101 + level_index)
        key_count, key_perm = jax.random.split(key_level, 2)
        refined = jax.random.randint(key_count, (device_count, 1), least_refined, most_refined + 1).astype(jnp.int32)
        own_count = refined + jnp.where(is_first, TAIL, 0).astype(jnp.int32)
        eligible = prev_live & (slot_index < boundary)
        shuffled = jax.vmap(lambda sub_key: jax.random.permutation(sub_key, SLOTS))(jax.random.split(key_perm, device_count)).astype(jnp.int32)
        scores = jnp.where(eligible, shuffled, -1)
        chosen_order = lax.top_k(scores, picked_count)[1].astype(jnp.int32)
        own_end = jnp.where(is_first, SLOTS, received_start).astype(jnp.int32)
        own_start = own_end - 8 * own_count
        in_own = (slot_index >= own_start) & (slot_index < own_end)
        rank = jnp.clip((slot_index - own_start) // 8, 0, picked_count - 1)
        own_parent = device_ids * SLOTS + jnp.take_along_axis(chosen_order, rank, axis=1)
        in_prev = (slot_index >= received_start) & (device_ids > 0)
        prev_parent = (device_ids - 1) * SLOTS + boundary + (slot_index - received_start) // 8
        octant = slot_index % 8
        link_rows = jnp.where(in_own, own_parent * 8 + octant, jnp.where(in_prev, prev_parent * 8 + octant, -1))
        levels_out.append(link_rows.reshape(-1).astype(jnp.int32))
        prev_live = in_own | in_prev
    return jnp.stack(levels_out, 0)


def levels(stream_key, shape, shards, low, top_value):
    def one(dim, parts):
        draws = jax.random.uniform(jax.random.fold_in(jax.random.fold_in(stream_key, 6), dim), (parts,), jnp.float32, low / len(shards), top_value / len(shards))
        return jnp.repeat(jnp.exp(draws), shape[dim] // parts).reshape((-1,) + (1,) * (len(shape) - dim - 1))

    level = one(*shards[0])
    for cut in shards[1:]:
        level = level * one(*cut)
    return level


def gaussian(own_key, shape, deviation, limit, shards=(), kind=jnp.bfloat16):
    factor_of = levels(own_key, shape, shards, -0.22, 0.18) if shards else 1.0
    entries = jax.random.normal(own_key, shape, jnp.float32) * deviation * factor_of
    return jnp.minimum(jnp.maximum(entries, -limit), limit).astype(kind)


def setup_inputs(seed: int = 0) -> dict:
    key_of = jax.random.split(jax.random.key(seed), 5)
    return {
        "coarse_scaling": gaussian(key_of[0], (K * K * K, BOXES), 1.0, 6.0, ((1, 1024),), jnp.float32),
        "details": gaussian(key_of[1], (LEVELS, 7 * K * K * K, BOXES), 1.0, 6.0, ((2, 1024),)),
        "two_scale": draw_two_scale(jax.random.fold_in(key_of[4], 71), 0),
        "parent_link": draw_parent_link(jax.random.fold_in(key_of[4], 71), 0),
    }


def unfilter(two_scale, scaling, wavelet):
    box_count = scaling.shape[1]
    poly_order = two_scale.shape[0] // 2
    coefficients = jnp.concatenate([scaling, wavelet], 0).reshape(2, 2, 2, poly_order, poly_order, poly_order, box_count)
    halves = two_scale.reshape(2, poly_order, 2, poly_order)
    precise = lax.Precision.HIGHEST
    first_pass = jnp.einsum("PIai,abcijkn->PIbcjkn", halves, coefficients, precision=precise)
    second_pass = jnp.einsum("QJbj,PIbcjkn->PIQJckn", halves, first_pass, precision=precise)
    third_pass = jnp.einsum("RMck,PIQJckn->IJMnPQR", halves, second_pass, precision=precise)
    return third_pass.reshape(poly_order * poly_order * poly_order, box_count * 8)


def reference(coarse_scaling, details, two_scale, parent_link):
    devices = BOXES // SLOTS
    cube_size = K * K * K
    scaling = coarse_scaling
    for level_index in range(LEVELS):
        scaling_blocks = scaling.reshape(cube_size, devices, SLOTS).transpose(1, 0, 2)
        wavelet_blocks = details[level_index].reshape(7 * cube_size, devices, SLOTS).transpose(1, 0, 2)
        link_blocks = parent_link[level_index].reshape(devices, SLOTS)
        device_ids = jnp.arange(devices, dtype=jnp.int32)

        def per_device(previous, inputs):
            block_scaling, block_wavelet, block_links, device = inputs
            own_children = unfilter(two_scale, block_scaling, block_wavelet.astype(jnp.float32))
            candidates = jnp.concatenate([previous, own_children], 1)
            position = block_links - (device - 1) * (SLOTS * 8)
            picked = jnp.take(candidates, jnp.clip(position, 0, 16 * SLOTS - 1), axis=1)
            return own_children, jnp.where(block_links[None, :] >= 0, picked, 0.0)

        initial = jnp.zeros((cube_size, 8 * SLOTS), jnp.float32)
        _, gathered = lax.scan(per_device, initial, (scaling_blocks, wavelet_blocks, link_blocks, device_ids))
        scaling = gathered.transpose(1, 0, 2).reshape(cube_size, BOXES)
    return scaling
```

```python
import jax
import jax.numpy as jnp
from jax import lax
from jax.experimental import pallas as pl
from jax.experimental.pallas import tpu as pltpu
from jax.sharding import PartitionSpec as P

MESH = pl.DeviceIdType.MESH
TAIL = 4
F32, BF16, I32 = jnp.float32, jnp.bfloat16, jnp.int32


def iota(shape, axis):
    return lax.broadcasted_iota(I32, shape, axis)


def nn(a, b):
    return lax.dot_general(a, b, (((1,), (0,)), ((), ())), preferred_element_type=F32)


def nt(a, b):
    return lax.dot_general(a, b, (((1,), (1,)), ((), ())), preferred_element_type=F32)


def split(x):
    hi = x.astype(BF16)
    return hi, (x - hi.astype(F32)).astype(BF16)


def triple(dot, a, b):
    return dot(a[0], b[0]) + dot(a[1], b[0]) + dot(a[0], b[1])


def flag(mask):
    return jnp.where(mask, 1.0, 0.0)


def one_hot(mask):
    return flag(mask).astype(BF16)


def pick_exact(dot, parts, other):
    return dot(parts[0], other) + dot(parts[1], other) + dot(parts[2], other)


def thirds(x):
    hi, rest = x.astype(BF16), None
    rest = x - hi.astype(F32)
    mid = rest.astype(BF16)
    return hi, mid, (rest - mid.astype(F32)).astype(BF16)


def kernel(
    leafs, subs,
    coarse_hbm, details_hbm, w_ref, link_ref, out_ref,
    coarse, details, x_hi, x_lo, x2, as_hi, as_lo, send0, recv0, send1, recv1, send2, recv2,
    local_sem, send_sem, recv_sem,
):
    leaf, sub = lax.axis_index("leaf"), lax.axis_index("sub")
    device = leaf * subs + sub
    total = leafs * subs
    ahead = lax.rem(device + 1, total)
    behind = lax.rem(device + total - 1, total)
    target = (lax.div(ahead, subs), lax.rem(ahead, subs))
    source = (lax.div(behind, subs), lax.rem(behind, subs))

    load_coarse = pltpu.make_async_copy(coarse_hbm, coarse, local_sem.at[0])
    load_first = pltpu.make_async_copy(details_hbm.at[0], details.at[0], local_sem.at[1])
    load_second = pltpu.make_async_copy(details_hbm.at[1], details.at[1], local_sem.at[2])
    load_coarse.start()
    load_first.start()
    load_second.start()

    barrier = pltpu.get_barrier_semaphore()
    pl.semaphore_signal(barrier, inc=1, device_id=source, device_id_type=MESH)

    first_child = device * 1024
    slot = iota((1, 128), 1)

    def read_links(level):
        link = link_ref[level : level + 1, :]
        live = link >= 0
        own = link >= first_child
        offset = link - first_child
        parent = jnp.where(own, offset, offset + 8 * TAIL) >> 3
        octant = link & 7
        group = (slot - octant) >> 3
        return live, own, live & (link < first_child), parent, octant, group

    def parents_of(links):
        live, own, before, parent, octant, group = links
        start = own & (octant == 0)
        lead = one_hot(((slot >> 3) == iota((16, 128), 0)) & start)
        match = one_hot(iota((128, 128), 0) == parent)
        return nt(lead, match)

    links1, links2 = read_links(0), read_links(1)
    row32 = iota((16, 128), 0)
    tail_rows = (iota((16, 128), 1) == 128 - TAIL + (row32 & 3))
    chosen1, chosen2 = parents_of(links1), parents_of(links2)
    twice = flag(tail_rows & (row32 < 8))
    once = flag(tail_rows & (row32 < 4))
    pick1 = jnp.concatenate([chosen1, twice], 0).astype(BF16)
    pick2 = jnp.concatenate([chosen2, twice], 0).astype(BF16)
    slots2 = jnp.concatenate([chosen2, once], 0).astype(BF16)

    upper = iota((8, 256), 0) < 4

    def stacked(level, a, i):
        first = 64 * i
        return [details[level, pl.ds(512 * (4 * a + q - 1) + first, 64), :] for q in range(4) if 4 * a + q]

    load_coarse.wait()
    load_first.wait()
    no_rows = jnp.zeros((192, 128), BF16)
    pick1_twice = jnp.concatenate([pick1, pick1], 1)
    for i in range(8):
        hi, lo = split(coarse[pl.ds(64 * i, 64), :])
        blocks = jnp.concatenate([hi] + stacked(0, 0, i), 0)
        lower = jnp.concatenate([lo, no_rows], 0)
        even = nt(pick1_twice, jnp.concatenate([blocks, lower], 1))
        odd = nt(pick1, jnp.concatenate(stacked(0, 1, i), 0))
        e_hi, e_lo = split(even[:16])
        x_hi[pl.ds(16 * i, 16), :] = e_hi
        x_lo[pl.ds(16 * i, 16), :] = e_lo
        x_hi[pl.ds(128 + 16 * i, 16), :] = odd[:16].astype(BF16)
        send0[pl.ds(8 * i, 8), :] = jnp.where(upper, even[16:24], odd[16:24])

    def hop(n, src, dst):
        return pltpu.make_async_remote_copy(
            src_ref=src, dst_ref=dst, send_sem=send_sem.at[n], recv_sem=recv_sem.at[n],
            device_id=target, device_id_type=MESH,
        )

    hop0, hop1, hop2 = hop(0, send0, recv0), hop(1, send1, recv1), hop(2, send2, recv2)
    pl.semaphore_wait(barrier, 1)
    hop0.start()

    load_second.wait()
    for i in range(8):
        even = nt(pick2, jnp.concatenate([jnp.zeros((64, 128), BF16)] + stacked(1, 0, i), 0))
        odd = nt(pick2, jnp.concatenate(stacked(1, 1, i), 0))
        x2[pl.ds(16 * i, 16), :] = even[:16].astype(BF16)
        x2[pl.ds(128 + 16 * i, 16), :] = odd[:16].astype(BF16)
        send1[pl.ds(8 * i, 8), :] = jnp.where(upper, even[16:24], odd[16:24])
    hop1.start()

    w = w_ref[...]
    w_parts = thirds(w)
    r16, l16 = iota((256, 16), 0), iota((256, 16), 1)
    at_outer = one_hot(l16 == ((r16 >> 7) << 3) + ((r16 >> 3) & 7))
    at_inner = one_hot(l16 == (((r16 >> 6) & 1) << 3) + (r16 & 7))

    def spread(at):
        rows = nn(at, w_parts[0]) + nn(at, w_parts[1]) + nn(at, w_parts[2])
        return pick_exact(nt, thirds(rows), at)

    kw = split(spread(at_outer) * spread(at_inner))
    w_hi, w_lo = w_parts[0], w_parts[1]

    live1, own1, before1, parent1, octant1, group1 = links1
    att = iota((64, 128), 0)
    traits = (
        (own1 & (att == group1))
        | (before1 & (att == 16 + parent1))
        | (live1 & (att == 20 + (octant1 >> 2)))
        | (live1 & (att == 24 + (octant1 & 3)))
    )
    boxes = nt(slots2, one_hot(traits)).astype(BF16)
    rho, box = iota((160, 32), 0), iota((160, 32), 1)
    is_tail = rho >= 128
    rows_of = jnp.where(is_tail, 16 + (rho & 3), rho & 15)
    per_row = nn(one_hot(box == rows_of), boxes).astype(BF16)
    trait, col = iota((64, 768), 0), iota((64, 768), 1)
    prev_col, qr_col = col - 256, col - 384
    table = (
        ((col < 256) & (trait == (col & 15)))
        | ((col >= 256) & (col < 320) & (trait == 16 + (prev_col & 3)))
        | ((col >= 384) & (col < 640) & (trait == 24 + (qr_col >> 6)))
        | ((col >= 640) & (col < 656) & (trait == 20 + ((col - 640) >> 3)))
    )
    masks = nn(per_row, one_hot(table))
    rho16, y16 = iota((160, 128), 0), iota((160, 128), 1)
    own_index = jnp.where(rho16 >= 128, (rho16 - 128) >> 2, rho16 >> 4)
    choose = jnp.where((y16 & 7) == own_index, masks[:, 640:768], 0.0).astype(BF16)
    x384, c384 = iota((16, 384), 0), iota((16, 384), 1)
    p384 = c384 - 256
    fine = jnp.where(c384 < 256, c384 >> 4, (((p384 >> 2) & 1) << 3) + (p384 >> 3))
    columns = one_hot(x384 == fine)
    pad = jnp.zeros((112, 384), BF16)
    keep = masks[:, :384]

    def lifted(part):
        wide = jnp.concatenate([nn(part, columns).astype(BF16), pad], 0)
        return (nn(choose, wide) * keep).astype(BF16)

    up_hi, up_lo = lifted(w_hi), lifted(w_lo)
    own_up = (up_hi[:, :256], up_lo[:, :256])
    prev_up = (up_hi[:, 256:320], up_lo[:, 256:320])
    y1 = nt(x_hi[...], kw[0]) + nt(x_hi[...], kw[1])
    y1 = y1 + jnp.concatenate([nt(x_lo[...], kw[0]), jnp.zeros((128, 256), F32)], 0)
    v = triple(nn, own_up, split(y1))

    live2, own2, before2, parent2, octant2, group2 = links2
    row320, x320 = iota((320, 16), 0), iota((320, 16), 1)
    q320 = row320 - 256
    fine = jnp.where(row320 < 256, row320 >> 4, (((q320 >> 2) & 1) << 3) + (q320 >> 3))
    at_fine = one_hot(x320 == fine)
    down = (nt(at_fine, w_hi).astype(BF16), nt(at_fine, w_lo).astype(BF16))
    rows = iota((320, 128), 0)
    mine = ((rows < 256) & own2 & ((rows & 15) == group2)) | ((rows >= 256) & before2 & ((rows & 3) == parent2))
    y128 = iota((16, 128), 0)
    for i in range(8):
        which = one_hot(live2 & (y128 == ((octant2 >> 2) << 3) + i))
        as_hi[:, pl.ds(128 * i, 128)] = jnp.where(mine, nn(down[0], which), 0.0).astype(BF16)
        as_lo[:, pl.ds(128 * i, 128)] = jnp.where(mine, nn(down[1], which), 0.0).astype(BF16)

    det = nt(kw[0], x2[...]) + nt(kw[1], x2[...])
    quarter = [octant2 & 3 == q for q in range(4)]

    def gathered(block):
        parts = [jnp.where(quarter[q], block[64 * q : 64 * q + 64], 0.0) for q in range(4)]
        return (parts[0] + parts[1]) + (parts[2] + parts[3])

    hop0.wait_recv()
    tail_y = triple(nt, split(recv0[...]), kw)
    v = v + triple(nn, prev_up, split(tail_y))
    v = v * masks[:, 384:640]
    v = v[:, :128] + v[:, 128:]
    send2[...] = v[128:160]
    hop2.start()

    base = tuple(jnp.concatenate([k[:, :64], k[:, :64]], 1) for k in kw)
    own_scaled = triple(nt, base, split(v[:128]))
    y2 = split(jnp.concatenate([det[:, :128] + own_scaled, det[:, 128:]], 1))

    hop1.wait_recv()
    tail2 = recv1[...].astype(BF16)
    tail_det = split(nt(kw[0], tail2) + nt(kw[1], tail2))
    for i in range(8):
        lanes = pl.ds(128 * i, 128)
        block = triple(nn, y2, (as_hi[0:256, lanes], as_lo[0:256, lanes]))
        block = block + triple(nn, tail_det, (as_hi[256:320, lanes], as_lo[256:320, lanes]))
        out_ref[pl.ds(64 * i, 64), :] = gathered(block)

    hop2.wait_recv()
    r64, c64 = iota((64, 32), 0), iota((64, 32), 1)
    place = one_hot(r64 == ((c64 >> 2) << 3) + (c64 & 3))
    last = triple(nt, base, split(recv2[...]))
    l_hi, l_lo = split(last)
    last = (nt(l_hi, place).astype(BF16), nt(l_lo, place).astype(BF16))
    for i in range(8):
        lanes = pl.ds(128 * i, 128)
        block = triple(nn, last, (as_hi[256:320, lanes], as_lo[256:320, lanes]))
        out_ref[pl.ds(64 * i, 64), :] += gathered(block)

    hop0.wait_send()
    hop1.wait_send()
    hop2.wait_send()


def solution(mesh):
    leafs, subs = mesh.shape["leaf"], mesh.shape["sub"]

    def on_device(coarse_scaling, details, two_scale, parent_link):
        anywhere = pl.BlockSpec(memory_space=pl.ANY)
        inside = pl.BlockSpec(memory_space=pltpu.VMEM)
        tail = pltpu.VMEM((64, 256), F32)
        return pl.pallas_call(
            lambda *refs: kernel(leafs, subs, *refs),
            out_shape=jax.ShapeDtypeStruct(coarse_scaling.shape, F32),
            in_specs=[anywhere, anywhere, inside, inside],
            out_specs=inside,
            scratch_shapes=[
                pltpu.VMEM(coarse_scaling.shape, F32),
                pltpu.VMEM(details.shape, BF16),
                pltpu.VMEM((256, 256), BF16),
                pltpu.VMEM((128, 256), BF16),
                pltpu.VMEM((256, 256), BF16),
                pltpu.VMEM((320, 1024), BF16),
                pltpu.VMEM((320, 1024), BF16),
                tail, tail, tail, tail,
                pltpu.VMEM((32, 128), F32),
                pltpu.VMEM((32, 128), F32),
                pltpu.SemaphoreType.DMA((3,)),
                pltpu.SemaphoreType.DMA((3,)),
                pltpu.SemaphoreType.DMA((3,)),
            ],
            compiler_params=pltpu.CompilerParams(collective_id=0, has_side_effects=True),
            name="reconstruct",
        )(coarse_scaling, details, two_scale, parent_link)

    placed = (
        P(None, ("leaf", "sub")),
        P(None, None, ("leaf", "sub")),
        P(),
        P(None, ("leaf", "sub")),
    )
    return jax.shard_map(
        on_device, mesh=mesh, in_specs=placed, out_specs=P(None, ("leaf", "sub")), check_vma=False
    )
```

```python
import jax
import jax.numpy as jnp
from jax import lax
from jax.experimental import pallas as pl
from jax.experimental.pallas import tpu as pltpu
from jax.sharding import PartitionSpec as P

MESH = pl.DeviceIdType.MESH
TAIL = 4
F32, BF16, I32 = jnp.float32, jnp.bfloat16, jnp.int32


def iota(shape, axis):
    return lax.broadcasted_iota(I32, shape, axis)


def nn(a, b):
    return lax.dot_general(a, b, (((1,), (0,)), ((), ())), preferred_element_type=F32)


def nt(a, b):
    return lax.dot_general(a, b, (((1,), (1,)), ((), ())), preferred_element_type=F32)


def split(x):
    hi = x.astype(BF16)
    return hi, (x - hi.astype(F32)).astype(BF16)


def triple(dot, a, b):
    return dot(a[0], b[0]) + dot(a[1], b[0]) + dot(a[0], b[1])


def flag(mask):
    return jnp.where(mask, 1.0, 0.0)


def one_hot(mask):
    return flag(mask).astype(BF16)


def kernel(
    leafs, subs,
    coarse_hbm, details_hbm, w_hbm, link_hbm, out_ref,
    coarse, details, w_ref, link_ref, x_hi, x_lo, x2, as_hi, as_lo, mixed,
    up_hi, up_lo, quarter, p_hi, p_lo,
    send0, recv0, send1, recv1, send2, recv2, local_sem, send_sem, recv_sem,
):
    leaf, sub = lax.axis_index("leaf"), lax.axis_index("sub")
    device = leaf * subs + sub
    total = leafs * subs
    ahead = lax.rem(device + 1, total)
    behind = lax.rem(device + total - 1, total)
    target = (lax.div(ahead, subs), lax.rem(ahead, subs))
    source = (lax.div(behind, subs), lax.rem(behind, subs))
    has_source, has_target = device > 0, device < total - 1
    patient = sub < 2

    def load(n, src, dst):
        copy = pltpu.make_async_copy(src, dst, local_sem.at[n])
        copy.start()
        return copy

    load_link = load(0, link_hbm, link_ref)
    load_coarse = load(1, coarse_hbm, coarse)
    load_w = load(2, w_hbm, w_ref)
    load_first = []
    for c in range(4):
        rows = pl.ds(128 * c, 128)
        load_first.append(load(4 + c, details_hbm.at[0, :, rows, :], details.at[0, :, rows, :]))
    load_second = load(3, details_hbm.at[1], details.at[1])

    barrier = pltpu.get_barrier_semaphore()

    @pl.when(has_source)
    def _():
        pl.semaphore_signal(barrier, inc=1, device_id=source, device_id_type=MESH)

    def hop(n, src, dst):
        return pltpu.make_async_remote_copy(
            src_ref=src, dst_ref=dst, send_sem=send_sem.at[n], recv_sem=recv_sem.at[n],
            device_id=target, device_id_type=MESH,
        )

    hop0 = [hop(2 + c, send0.at[pl.ds(16 * c, 16), :], recv0.at[pl.ds(16 * c, 16), :]) for c in range(4)]
    hop1, hop2 = hop(0, send1, recv1), hop(1, send2, recv2)

    def fine(row):
        return (((row >> 3) & 1) << 3) + ((row >> 4) << 1) + ((row >> 2) & 1)

    first_child = device * 1024
    slot = iota((1, 128), 1)
    load_link.wait()

    def read_links(level):
        link = link_ref[level : level + 1, :]
        live = link >= 0
        own = link >= first_child
        offset = link - first_child
        parent = jnp.where(own, offset, offset + 8 * TAIL) >> 3
        octant = link & 7
        group = (slot - octant) >> 3
        return live, own, live & (link < first_child), parent, octant, group

    def parents_of(links):
        live, own, before, parent, octant, group = links
        start = own & (octant == 0)
        lead = one_hot(((slot >> 3) == iota((16, 128), 0)) & start)
        match = one_hot(iota((128, 128), 0) == parent)
        return nt(lead, match)

    links1, links2 = read_links(0), read_links(1)
    r16, s16 = iota((16, 128), 0), iota((16, 128), 1)
    tails = flag((r16 < 8) & (s16 == 128 - TAIL + (r16 & 3)))
    chosen1, chosen2 = parents_of(links1), parents_of(links2)
    pick1 = jnp.concatenate([chosen1, tails], 0).astype(BF16)
    pick2 = jnp.concatenate([chosen2, tails], 0).astype(BF16)

    upper = iota((8, 256), 0) < 4

    def stacked(level, a, i):
        first = 64 * i
        return [details[level, 4 * a + q - 1, pl.ds(first, 64), :] for q in range(4) if 4 * a + q]

    load_coarse.wait()
    no_rows = jnp.zeros((192, 128), BF16)
    pick1_twice = jnp.concatenate([pick1, pick1], 1)
    held = [None, None]
    for i in range(8):
        if i % 2 == 0:
            load_first[i // 2].wait()
        hi, lo = split(coarse[pl.ds(64 * i, 64), :])
        blocks = jnp.concatenate([hi] + stacked(0, 0, i), 0)
        lower = jnp.concatenate([lo, no_rows], 0)
        even = nt(pick1_twice, jnp.concatenate([blocks, lower], 1))
        odd = nt(pick1, jnp.concatenate(stacked(0, 1, i), 0))
        e_hi, e_lo = split(even[:16])
        x_hi[pl.ds(16 * i, 16), :] = e_hi
        x_lo[pl.ds(16 * i, 16), :] = e_lo
        x_hi[pl.ds(128 + 16 * i, 16), :] = odd[:16].astype(BF16)
        if i % 2:
            send0[pl.ds(8 * i - 8, 8), :] = jnp.where(upper, held[0], even[16:24])
            send0[pl.ds(8 * i, 8), :] = jnp.where(upper, held[1], odd[16:24])

            @pl.when(has_target & ~patient)
            def _(c=i // 2):
                if c == 0:
                    pl.semaphore_wait(barrier, 1)
                hop0[c].start()

        held = [even[16:24], odd[16:24]]

    load_second.wait()
    for i in range(8):
        even = nt(pick2, jnp.concatenate([jnp.zeros((64, 128), BF16)] + stacked(1, 0, i), 0))
        odd = nt(pick2, jnp.concatenate(stacked(1, 1, i), 0))
        x2[pl.ds(16 * i, 16), :] = even[:16].astype(BF16)
        x2[pl.ds(128 + 16 * i, 16), :] = odd[:16].astype(BF16)
        if i % 2:
            send1[pl.ds(8 * i - 8, 8), :] = jnp.where(upper, held[0], even[16:24])
            send1[pl.ds(8 * i, 8), :] = jnp.where(upper, held[1], odd[16:24])
        held = [even[16:24], odd[16:24]]

    @pl.when(has_target & ~patient)
    def _():
        hop1.start()

    load_w.wait()
    w = w_ref[...]
    w_hi, w_lo = split(w)
    row, lane = iota((256, 32), 0), iota((256, 32), 1)
    at_outer = one_hot((lane & 15) == ((row >> 7) << 3) + ((row >> 3) & 7))
    at_inner = one_hot((lane & 15) == (((row >> 6) & 1) << 3) + (row & 7))
    tall = jnp.concatenate([w_hi, w_lo], 0)
    wide = jnp.concatenate([tall, tall], 1)

    def spread(at):
        rows = nn(at, wide)
        top = rows.astype(BF16).astype(F32)
        return nt(jnp.where(lane < 16, top, rows - top).astype(BF16), at)

    kw = split(spread(at_outer) * spread(at_inner))

    live1, own1, before1, parent1, octant1, group1 = links1
    turned = jnp.concatenate([w[8:16], w[0:8]], 0)
    t_hi, t_lo = split(turned)
    x192, c192 = iota((16, 192), 0), iota((16, 192), 1)
    fits = x192 == fine(c192 & 63)
    middle = (c192 >> 6) == 1
    lift = nn(t_hi, one_hot(fits & ~middle)) + nn(t_lo, one_hot(fits & middle))
    lift = jnp.where((c192 & 3) == parent1[:, 127:128], lift, 0.0).astype(BF16)

    live2, own2, before2, parent2, octant2, group2 = links2
    base = tuple(jnp.concatenate([k[:, :64], k[:, :64]], 1) for k in kw)

    def folded(block, quarters):
        parts = [jnp.where(quarters == q, block[64 * q : 64 * q + 64], 0.0) for q in range(4)]
        return (parts[0] + parts[1]) + (parts[2] + parts[3])

    def own_work():
        att = iota((64, 128), 0)
        traits = (
            (own1 & (att == group1))
            | (before1 & (att == 16 + parent1))
            | (live1 & (att == 20 + (octant1 >> 2)))
            | (live1 & (att == 24 + (octant1 & 3)))
        )
        boxes = nt(chosen2.astype(BF16), one_hot(traits)).astype(BF16)
        per_row = nn(one_hot(iota((128, 16), 1) == (iota((128, 16), 0) & 15)), boxes).astype(BF16)
        trait, col = iota((64, 768), 0), iota((64, 768), 1)
        table = (
            ((col < 256) & (trait == (col & 15)))
            | ((col >= 256) & (col < 320) & (trait == 16 + (col & 3)))
            | ((col >= 384) & (col < 640) & (trait == 24 + ((col - 384) >> 6)))
            | ((col >= 640) & (col < 656) & (trait == 20 + ((col - 640) >> 3)))
        )
        masks = nn(per_row, one_hot(table))
        rho, y128 = iota((128, 128), 0), iota((128, 128), 1)
        choose = jnp.where((y128 & 7) == (rho >> 4), masks[:, 640:768], 0.0).astype(BF16)
        x384, c384 = iota((16, 384), 0), iota((16, 384), 1)
        columns = one_hot(x384 == jnp.where(c384 < 256, c384 >> 4, fine(c384 - 256)))
        pad = jnp.zeros((112, 384), BF16)
        keep = masks[:, :384]

        def lifted(part):
            rows = jnp.concatenate([nn(part, columns).astype(BF16), pad], 0)
            return (nn(choose, rows) * keep).astype(BF16)

        raised = lifted(w_hi), lifted(w_lo)
        up_hi[...], up_lo[...] = raised[0][:, 256:], raised[1][:, 256:]
        quarter[...] = masks[:, 384:640]
        own_up = (raised[0][:, :256], raised[1][:, :256])
        y1 = nt(x_hi[...], kw[0]) + nt(x_hi[...], kw[1])
        y1 = y1 + jnp.concatenate([nt(x_lo[...], kw[0]), jnp.zeros((128, 256), F32)], 0)
        v = triple(nn, own_up, split(y1)) * masks[:, 384:640]
        v = v[:, :128] + v[:, 128:]

        at_fine = one_hot(iota((256, 16), 1) == (iota((256, 16), 0) >> 4))
        down = (nt(at_fine, w_hi).astype(BF16), nt(at_fine, w_lo).astype(BF16))
        mine = own2 & ((iota((256, 128), 0) & 15) == group2)
        for i in range(8):
            which = one_hot(live2 & (r16 == ((octant2 >> 2) << 3) + i))
            as_hi[:, pl.ds(128 * i, 128)] = jnp.where(mine, nn(down[0], which), 0.0).astype(BF16)
            as_lo[:, pl.ds(128 * i, 128)] = jnp.where(mine, nn(down[1], which), 0.0).astype(BF16)

        det = nt(kw[0], x2[...]) + nt(kw[1], x2[...])
        own_scaled = triple(nt, base, split(v))
        y2 = split(jnp.concatenate([det[:, :128] + own_scaled, det[:, 128:]], 1))

        for i in range(8):
            lanes = pl.ds(128 * i, 128)
            block = triple(nn, y2, (as_hi[:, lanes], as_lo[:, lanes]))
            out_ref[pl.ds(64 * i, 64), :] = folded(block, octant2 & 3)

        names = one_hot(before2 & (parent2 == r16))
        c128 = iota((128, 256), 1)
        named = nn(names, one_hot(iota((128, 256), 0) == 96 + (c128 & 31))).astype(BF16)
        row96, x96 = iota((96, 16), 0), iota((96, 16), 1)
        late = row96 - 64
        comes = nn(one_hot(x96 == jnp.where(row96 < 64, row96 & 3, late >> 3)), named)
        at_prev = one_hot(x96 == jnp.where(row96 < 64, fine(row96 & 63), late & 7))
        c16 = iota((16, 256), 1)
        which = one_hot(iota((16, 256), 0) == (((c16 >> 2) & 1) << 3) + (c16 >> 5))

        def dropped(part):
            return (nn(nt(at_prev, part).astype(BF16), which) * comes).astype(BF16)

        p_hi[...], p_lo[...] = dropped(w_hi), dropped(w_lo)

    def messages():
        @pl.when(has_target & patient)
        def _():
            pl.semaphore_wait(barrier, 1)
            for copy in hop0:
                copy.start()
            hop1.start()

        @pl.when(has_source)
        def _():
            for copy in hop0:
                copy.wait_recv()
            hi, lo = split(recv0[...])
            mixed[...] = nn(lift, jnp.concatenate([hi, hi, lo], 0))[:8]

        @pl.when(device == 0)
        def _():
            recv0[...] = jnp.zeros((64, 256), F32)
            recv1[...] = jnp.zeros((64, 256), F32)
            recv2[...] = jnp.zeros((8, 256), F32)
            x256, c256 = iota((16, 256), 0), iota((16, 256), 1)
            fits = one_hot((x256 == (c256 >> 4)) & ((c256 & 15) == 15))
            l_hi, l_lo = nn(t_hi, fits).astype(BF16), nn(t_lo, fits).astype(BF16)
            both = nn(l_hi, x_hi[...]) + nn(l_lo, x_hi[...]) + nn(l_hi[:, :128], x_lo[...])
            mixed[...] = both[:8]

        @pl.when(has_target)
        def _():
            top = mixed[...].astype(BF16).astype(F32)
            pair = jnp.concatenate([top, mixed[...] - top], 0).astype(BF16)
            main = nt(pair, kw[0])
            send2[...] = main[:8] + main[8:] + nt(pair, kw[1])[:8]
            hop2.start()

    @pl.loop(0, 2)
    def _(n):
        turn = (n == 0) == patient
        pl.when(turn)(own_work)
        pl.when(jnp.logical_not(turn))(messages)

    tail_y = triple(nt, split(recv0[...]), kw)
    v = triple(nn, (up_hi[:, :64], up_lo[:, :64]), split(tail_y)) * quarter[...]
    v = v[:, :128] + v[:, 128:]
    s_hi, s_lo = split(triple(nt, base, split(v)))
    both = jnp.concatenate([s_hi, s_lo], 1)
    for i in range(8):
        lanes = pl.ds(128 * i, 128)
        top = as_hi[:128, lanes]
        block = nn(both, jnp.concatenate([top, top], 0)) + nn(s_hi, as_lo[:128, lanes])
        out_ref[pl.ds(64 * i, 64), :] += folded(block, octant2 & 3)

    scaled = jnp.concatenate([p_hi[64:, :], p_hi[64:, :], p_lo[64:, :]], 0)
    base4 = tuple(jnp.concatenate([b, b], 1) for b in base)
    static = iota((64, 256), 1) & 3
    reach = (iota((96, 256), 1) >> 6) == ((iota((96, 256), 0) >> 3) & 3)
    turn = iota((256, 96), 1) >> 5

    @pl.when(has_source)
    def _():
        hop1.wait_recv()
        tail2 = recv1[...].astype(BF16)
        tail_det = split(nt(kw[0], tail2) + nt(kw[1], tail2))
        prior = folded(triple(nn, tail_det, (p_hi[:64, :], p_lo[:64, :])), static)
        hop2.wait_recv()
        parts = split(jnp.where(reach, jnp.concatenate([recv2[...]] * 12, 0), 0.0))
        last = triple(nt, base4, parts)
        top = last.astype(BF16).astype(F32)
        block = nn(jnp.where(turn == 1, last - top, top).astype(BF16), scaled)
        block = prior + folded(block, static)
        for i in range(8):
            tile = block[:, 128 * (i // 4) : 128 * (i // 4) + 128]
            if i % 4 < 3:
                tile = pltpu.roll(tile, 96 - 32 * (i % 4), 1)
            rows = pl.ds(64 * i, 64)
            out_ref[rows, :] = jnp.where(before2, tile, out_ref[rows, :])

    @pl.when(has_target)
    def _():
        for copy in hop0 + [hop1, hop2]:
            copy.wait_send()


def solution(mesh):
    leafs, subs = mesh.shape["leaf"], mesh.shape["sub"]

    def on_device(coarse_scaling, details, two_scale, parent_link):
        outside = pl.BlockSpec(memory_space=pltpu.HBM)
        details = details.reshape(2, 7, 512, 128)
        tail = pltpu.VMEM((64, 256), F32)
        return pl.pallas_call(
            lambda *refs: kernel(leafs, subs, *refs),
            out_shape=jax.ShapeDtypeStruct(coarse_scaling.shape, F32),
            in_specs=[outside] * 4,
            out_specs=pl.BlockSpec(memory_space=pltpu.VMEM),
            scratch_shapes=[
                pltpu.VMEM(coarse_scaling.shape, F32),
                pltpu.VMEM(details.shape, BF16),
                pltpu.VMEM(two_scale.shape, F32),
                pltpu.VMEM(parent_link.shape, I32),
                pltpu.VMEM((256, 256), BF16),
                pltpu.VMEM((128, 256), BF16),
                pltpu.VMEM((256, 256), BF16),
                pltpu.VMEM((256, 1024), BF16),
                pltpu.VMEM((256, 1024), BF16),
                pltpu.VMEM((8, 256), F32),
                pltpu.VMEM((128, 128), BF16),
                pltpu.VMEM((128, 128), BF16),
                pltpu.VMEM((128, 256), F32),
                pltpu.VMEM((96, 256), BF16),
                pltpu.VMEM((96, 256), BF16),
                tail, tail, tail, tail,
                pltpu.VMEM((8, 256), F32),
                pltpu.VMEM((8, 256), F32),
                pltpu.SemaphoreType.DMA((8,)),
                pltpu.SemaphoreType.DMA((6,)),
                pltpu.SemaphoreType.DMA((6,)),
            ],
            compiler_params=pltpu.CompilerParams(
                collective_id=0, has_side_effects=True, vmem_limit_bytes=32 << 20
            ),
            name="reconstruct",
        )(*[pltpu.with_memory_space_constraint(a, pltpu.HBM) for a in (coarse_scaling, details, two_scale, parent_link)])

    placed = (
        P(None, ("leaf", "sub")),
        P(None, None, ("leaf", "sub")),
        P(),
        P(None, ("leaf", "sub")),
    )
    return jax.shard_map(
        on_device, mesh=mesh, in_specs=placed, out_specs=P(None, ("leaf", "sub")), check_vma=False
    )
```

```python
import jax
import jax.numpy as jnp
from jax import lax
from jax.experimental import pallas as pl
from jax.experimental.pallas import tpu as pltpu
from jax.sharding import PartitionSpec as P

MESH = pl.DeviceIdType.MESH
TAIL = 4
F32, BF16, I32 = jnp.float32, jnp.bfloat16, jnp.int32


def iota(shape, axis):
    return lax.broadcasted_iota(I32, shape, axis)


def nn(a, b):
    return lax.dot_general(a, b, (((1,), (0,)), ((), ())), preferred_element_type=F32)


def nt(a, b):
    return lax.dot_general(a, b, (((1,), (1,)), ((), ())), preferred_element_type=F32)


def split(x):
    hi = x.astype(BF16)
    return hi, (x - hi.astype(F32)).astype(BF16)


def triple(dot, a, b):
    if a[0].shape[1] != 128:
        return dot(a[0], b[0]) + dot(a[1], b[0]) + dot(a[0], b[1])
    doubled = jnp.concatenate([b[0], b[0]], 0 if dot is nn else 1)
    return dot(jnp.concatenate([a[0], a[1]], 1), doubled) + dot(a[0], b[1])


def below(x, rows):
    return jnp.concatenate([x, jnp.zeros((rows, x.shape[1]), x.dtype)], 0)


def flag(mask):
    return jnp.where(mask, 1.0, 0.0)


def one_hot(mask):
    return flag(mask).astype(BF16)


def kernel(
    leafs, subs,
    coarse_hbm, details_hbm, w_hbm, link_hbm, out_ref,
    coarse, details, w_ref, link_ref, x_hi, x_lo, x2, as_hi, as_lo, mixed,
    up_hi, up_lo, quarter, p_hi, p_lo,
    send0, recv0, send1, recv1, send2, recv2, local_sem, send_sem, recv_sem,
):
    leaf, sub = lax.axis_index("leaf"), lax.axis_index("sub")
    device = leaf * subs + sub
    total = leafs * subs
    ahead = lax.rem(device + 1, total)
    behind = lax.rem(device + total - 1, total)
    target = (lax.div(ahead, subs), lax.rem(ahead, subs))
    source = (lax.div(behind, subs), lax.rem(behind, subs))
    has_source, has_target = device > 0, device < total - 1
    patient = sub < 2

    def load(n, src, dst):
        copy = pltpu.make_async_copy(src, dst, local_sem.at[n])
        copy.start()
        return copy

    load_link = load(0, link_hbm, link_ref)
    load_coarse = load(1, coarse_hbm, coarse)
    load_w = load(2, w_hbm, w_ref)
    load_first = []
    for c in range(4):
        rows = pl.ds(128 * c, 128)
        load_first.append(load(4 + c, details_hbm.at[0, :, rows, :], details.at[0, :, rows, :]))
    load_second = load(3, details_hbm.at[1], details.at[1])

    barrier = pltpu.get_barrier_semaphore()

    @pl.when(has_source)
    def _():
        pl.semaphore_signal(barrier, inc=1, device_id=source, device_id_type=MESH)

    def hop(n, src, dst):
        return pltpu.make_async_remote_copy(
            src_ref=src, dst_ref=dst, send_sem=send_sem.at[n], recv_sem=recv_sem.at[n],
            device_id=target, device_id_type=MESH,
        )

    hop0 = [hop(2 + c, send0.at[pl.ds(16 * c, 16), :], recv0.at[pl.ds(16 * c, 16), :]) for c in range(4)]
    hop1, hop2 = hop(0, send1, recv1), hop(1, send2, recv2)

    def fine(row):
        return (((row >> 3) & 1) << 3) + ((row >> 4) << 1) + ((row >> 2) & 1)

    first_child = device * 1024
    slot = iota((1, 128), 1)
    load_link.wait()

    def read_links(level):
        link = link_ref[level : level + 1, :]
        live = link >= 0
        own = link >= first_child
        offset = link - first_child
        parent = jnp.where(own, offset, offset + 8 * TAIL) >> 3
        octant = link & 7
        group = (slot - octant) >> 3
        return live, own, live & (link < first_child), parent, octant, group

    def parents_of(links):
        live, own, before, parent, octant, group = links
        start = own & (octant == 0)
        lead = one_hot(((slot >> 3) == iota((16, 128), 0)) & start)
        match = one_hot(iota((128, 128), 0) == parent)
        return nt(lead, match)

    links1, links2 = read_links(0), read_links(1)
    r16, s16 = iota((16, 128), 0), iota((16, 128), 1)
    tails = flag((r16 < 8) & (s16 == 128 - TAIL + (r16 & 3)))
    chosen1, chosen2 = parents_of(links1), parents_of(links2)
    pick1 = jnp.concatenate([chosen1, tails], 0).astype(BF16)
    pick2 = jnp.concatenate([chosen2, tails], 0).astype(BF16)

    upper = iota((8, 256), 0) < 4

    def stacked(level, a, i):
        first = 64 * i
        return [details[level, 4 * a + q - 1, pl.ds(first, 64), :] for q in range(4) if 4 * a + q]

    load_coarse.wait()
    first_half = iota((32, 128), 1) < 64

    def parents_blocks(c):
        hi, lo = split(coarse[pl.ds(128 * c, 128), :])
        finer = nt(pick1, lo)
        pairs = []
        for n in range(2):
            i = 2 * c + n
            even = nt(pick1, jnp.concatenate([hi[64 * n : 64 * n + 64]] + stacked(0, 0, i), 0))
            rest = jnp.where(first_half, pltpu.roll(finer, 64, 1) if n else finer, 0.0)
            even = jnp.concatenate([even[:, :128] + rest, even[:, 128:]], 1)
            pairs.append((even, nt(pick1, jnp.concatenate(stacked(0, 1, i), 0))))
        return pairs

    def keep_piece(c, pairs):
        for i, (even, odd) in zip((2 * c, 2 * c + 1), pairs):
            e_hi, e_lo = split(even[:16])
            x_hi[pl.ds(16 * i, 16), :] = e_hi
            x_lo[pl.ds(16 * i, 16), :] = e_lo
            x_hi[pl.ds(128 + 16 * i, 16), :] = odd[:16].astype(BF16)

    def send_piece(c, pairs):
        for half in range(2):
            first, second = pairs[0][half], pairs[1][half]
            send0[pl.ds(16 * c + 8 * half, 8), :] = jnp.where(upper, first[16:24], second[16:24])

        @pl.when(has_target & ~patient)
        def _():
            if c == 0:
                pl.semaphore_wait(barrier, 1)
            hop0[c].start()

    pieces = []
    for c in range(4):
        load_first[c].wait()
        pieces.append(parents_blocks(c))
        if c:
            send_piece(c - 1, pieces[c - 1])
    send_piece(3, pieces[3])
    for c in range(4):
        keep_piece(c, pieces[c])

    load_second.wait()
    held = [None, None]
    for i in range(8):
        even = nt(pick2, jnp.concatenate([jnp.zeros((64, 128), BF16)] + stacked(1, 0, i), 0))
        odd = nt(pick2, jnp.concatenate(stacked(1, 1, i), 0))
        x2[pl.ds(16 * i, 16), :] = even[:16].astype(BF16)
        x2[pl.ds(128 + 16 * i, 16), :] = odd[:16].astype(BF16)
        if i % 2:
            send1[pl.ds(8 * i - 8, 8), :] = jnp.where(upper, held[0], even[16:24])
            send1[pl.ds(8 * i, 8), :] = jnp.where(upper, held[1], odd[16:24])
        held = [even[16:24], odd[16:24]]

    @pl.when(has_target & ~patient)
    def _():
        hop1.start()

    load_w.wait()
    w = w_ref[...]
    w_hi, w_lo = split(w)
    row, lane = iota((256, 32), 0), iota((256, 32), 1)
    at_outer = one_hot((lane & 15) == ((row >> 7) << 3) + ((row >> 3) & 7))
    at_inner = one_hot((lane & 15) == (((row >> 6) & 1) << 3) + (row & 7))
    tall = jnp.concatenate([w_hi, w_lo], 0)
    wide = jnp.concatenate([tall, tall], 1)

    def spread(at):
        rows = nn(at, wide)
        top = rows.astype(BF16).astype(F32)
        return nt(jnp.where(lane < 16, top, rows - top).astype(BF16), at)

    kw = split(spread(at_outer) * spread(at_inner))

    live1, own1, before1, parent1, octant1, group1 = links1
    turned = jnp.concatenate([w[8:16], w[0:8]], 0)
    t_hi, t_lo = split(turned)
    x192, c192 = iota((16, 192), 0), iota((16, 192), 1)
    fits = x192 == fine(c192 & 63)
    middle = (c192 >> 6) == 1
    lift = nn(t_hi, one_hot(fits & ~middle)) + nn(t_lo, one_hot(fits & middle))
    lift = jnp.where((c192 & 3) == parent1[:, 127:128], lift, 0.0).astype(BF16)

    live2, own2, before2, parent2, octant2, group2 = links2
    base = tuple(jnp.concatenate([k[:, :64], k[:, :64]], 1) for k in kw)

    def folded(block, quarters):
        parts = [jnp.where(quarters == q, block[64 * q : 64 * q + 64], 0.0) for q in range(4)]
        return (parts[0] + parts[1]) + (parts[2] + parts[3])

    def own_work():
        att = iota((64, 128), 0)
        traits = (
            (own1 & (att == group1))
            | (before1 & (att == 16 + parent1))
            | (live1 & (att == 20 + (octant1 >> 2)))
            | (live1 & (att == 24 + (octant1 & 3)))
        )
        boxes = nt(chosen2.astype(BF16), one_hot(traits)).astype(BF16)
        per_row = nn(one_hot(iota((128, 16), 1) == (iota((128, 16), 0) & 15)), boxes).astype(BF16)
        trait, col = iota((64, 768), 0), iota((64, 768), 1)
        table = (
            ((col < 256) & (trait == (col & 15)))
            | ((col >= 256) & (col < 320) & (trait == 16 + (col & 3)))
            | ((col >= 384) & (col < 640) & (trait == 24 + ((col - 384) >> 6)))
            | ((col >= 640) & (col < 656) & (trait == 20 + ((col - 640) >> 3)))
        )
        masks = nn(per_row, one_hot(table))
        rho, y128 = iota((128, 128), 0), iota((128, 128), 1)
        choose = jnp.where((y128 & 7) == (rho >> 4), masks[:, 640:768], 0.0).astype(BF16)
        x384, c384 = iota((16, 384), 0), iota((16, 384), 1)
        columns = one_hot(x384 == jnp.where(c384 < 256, c384 >> 4, fine(c384 - 256)))
        pad = jnp.zeros((112, 384), BF16)
        keep = masks[:, :384]

        def lifted(part):
            rows = jnp.concatenate([nn(part, columns).astype(BF16), pad], 0)
            return (nn(choose, rows) * keep).astype(BF16)

        raised = lifted(w_hi), lifted(w_lo)
        up_hi[...], up_lo[...] = raised[0][:, 256:], raised[1][:, 256:]
        quarter[...] = masks[:, 384:640]
        own_up = (raised[0][:, :256], raised[1][:, :256])
        y1 = nt(x_hi[...], kw[0]) + nt(x_hi[...], kw[1])
        y1 = y1 + below(nt(x_lo[...], kw[0]), 128)
        v = triple(nn, own_up, split(y1)) * masks[:, 384:640]
        v = v[:, :128] + v[:, 128:]

        at_fine = one_hot(iota((256, 16), 1) == (iota((256, 16), 0) >> 4))
        down = (nt(at_fine, w_hi).astype(BF16), nt(at_fine, w_lo).astype(BF16))
        mine = own2 & ((iota((256, 128), 0) & 15) == group2)
        for i in range(8):
            which = one_hot(live2 & (r16 == ((octant2 >> 2) << 3) + i))
            as_hi[:, pl.ds(128 * i, 128)] = jnp.where(mine, nn(down[0], which), 0.0).astype(BF16)
            as_lo[:, pl.ds(128 * i, 128)] = jnp.where(mine, nn(down[1], which), 0.0).astype(BF16)

        det = nt(kw[0], x2[...]) + nt(kw[1], x2[...])
        own_scaled = triple(nt, base, split(v))
        y2 = split(jnp.concatenate([det[:, :128] + own_scaled, det[:, 128:]], 1))

        for i in range(0, 8, 2):
            lanes = pl.ds(128 * i, 256)
            block = triple(nn, y2, (as_hi[:, lanes], as_lo[:, lanes]))
            for n in range(2):
                out_ref[pl.ds(64 * (i + n), 64), :] = folded(block[:, 128 * n : 128 * n + 128], octant2 & 3)

        names = one_hot(before2 & (parent2 == r16))
        c128 = iota((128, 256), 1)
        named = nn(names, one_hot(iota((128, 256), 0) == 96 + (c128 & 31))).astype(BF16)
        row96, x96 = iota((96, 16), 0), iota((96, 16), 1)
        late = row96 - 64
        comes = nn(one_hot(x96 == jnp.where(row96 < 64, row96 & 3, late >> 3)), named)
        at_prev = one_hot(x96 == jnp.where(row96 < 64, fine(row96 & 63), late & 7))
        c16 = iota((16, 256), 1)
        which = one_hot(iota((16, 256), 0) == (((c16 >> 2) & 1) << 3) + (c16 >> 5))

        def dropped(part):
            return (nn(nt(at_prev, part).astype(BF16), which) * comes).astype(BF16)

        p_hi[...], p_lo[...] = dropped(w_hi), dropped(w_lo)

    def messages():
        @pl.when(has_target & patient)
        def _():
            pl.semaphore_wait(barrier, 1)
            for copy in hop0:
                copy.start()
            hop1.start()

        @pl.when(has_source)
        def _():
            for copy in hop0:
                copy.wait_recv()
            hi, lo = split(recv0[...])
            mixed[...] = nn(lift, jnp.concatenate([hi, hi, lo], 0))[:8]

        @pl.when(device == 0)
        def _():
            recv0[...] = jnp.zeros((64, 256), F32)
            recv1[...] = jnp.zeros((64, 256), F32)
            recv2[...] = jnp.zeros((8, 256), F32)
            x256, c256 = iota((16, 256), 0), iota((16, 256), 1)
            fits = one_hot((x256 == (c256 >> 4)) & ((c256 & 15) == 15))
            l_hi, l_lo = nn(t_hi, fits).astype(BF16), nn(t_lo, fits).astype(BF16)
            both = nn(l_hi, x_hi[...]) + nn(l_lo, x_hi[...]) + nn(l_hi[:, :128], x_lo[...])
            mixed[...] = both[:8]

        @pl.when(has_target)
        def _():
            top = mixed[...].astype(BF16).astype(F32)
            pair = jnp.concatenate([top, mixed[...] - top], 0).astype(BF16)
            main = nt(pair, kw[0])
            send2[...] = main[:8] + main[8:] + nt(pair, kw[1])[:8]
            hop2.start()

    @pl.loop(0, 2)
    def _(n):
        turn = (n == 0) == patient
        pl.when(turn)(own_work)
        pl.when(jnp.logical_not(turn))(messages)

    tail_y = triple(nt, split(recv0[...]), kw)
    v = triple(nn, (up_hi[...], up_lo[...]), split(below(tail_y, 64))) * quarter[...]
    v = v[:, :128] + v[:, 128:]
    scaling = split(triple(nt, base, split(v)))
    for i in range(0, 8, 2):
        lanes = pl.ds(128 * i, 256)
        block = triple(nn, scaling, (as_hi[:128, lanes], as_lo[:128, lanes]))
        for n in range(2):
            out_ref[pl.ds(64 * (i + n), 64), :] += folded(block[:, 128 * n : 128 * n + 128], octant2 & 3)

    scaled = jnp.concatenate([p_hi[64:, :], p_hi[64:, :], p_lo[64:, :]], 0)
    static = iota((64, 256), 1) & 3
    reach = (iota((96, 128), 1) >> 6) == ((iota((96, 128), 0) >> 3) & 1)
    turn = iota((256, 96), 1) >> 5

    @pl.when(has_source)
    def _():
        hop1.wait_recv()
        tail2 = below(recv1[...].astype(BF16), 64)
        tail_det = split(nt(kw[0], tail2) + nt(kw[1], tail2))
        prior = folded(triple(nn, tail_det, (below(p_hi[:64, :], 64), below(p_lo[:64, :], 64))), static)
        hop2.wait_recv()
        left, right = recv2[:, :128], recv2[:, 128:]
        parts = split(jnp.where(reach, jnp.concatenate([left, left, right, right] * 3, 0), 0.0))
        last = triple(nt, base, parts)
        top = last.astype(BF16).astype(F32)
        block = nn(jnp.where(turn == 1, last - top, top).astype(BF16), scaled)
        block = prior + folded(block, static)
        for i in range(8):
            tile = block[:, 128 * (i // 4) : 128 * (i // 4) + 128]
            if i % 4 < 3:
                tile = pltpu.roll(tile, 96 - 32 * (i % 4), 1)
            rows = pl.ds(64 * i, 64)
            out_ref[rows, :] = jnp.where(before2, tile, out_ref[rows, :])

    @pl.when(has_target)
    def _():
        for copy in hop0 + [hop1, hop2]:
            copy.wait_send()


def solution(mesh):
    leafs, subs = mesh.shape["leaf"], mesh.shape["sub"]

    def on_device(coarse_scaling, details, two_scale, parent_link):
        outside = pl.BlockSpec(memory_space=pltpu.HBM)
        details = details.reshape(2, 7, 512, 128)
        tail = pltpu.VMEM((64, 256), F32)
        return pl.pallas_call(
            lambda *refs: kernel(leafs, subs, *refs),
            out_shape=jax.ShapeDtypeStruct(coarse_scaling.shape, F32),
            in_specs=[outside] * 4,
            out_specs=pl.BlockSpec(memory_space=pltpu.VMEM),
            scratch_shapes=[
                pltpu.VMEM(coarse_scaling.shape, F32),
                pltpu.VMEM(details.shape, BF16),
                pltpu.VMEM(two_scale.shape, F32),
                pltpu.VMEM(parent_link.shape, I32),
                pltpu.VMEM((256, 256), BF16),
                pltpu.VMEM((128, 256), BF16),
                pltpu.VMEM((256, 256), BF16),
                pltpu.VMEM((256, 1024), BF16),
                pltpu.VMEM((256, 1024), BF16),
                pltpu.VMEM((8, 256), F32),
                pltpu.VMEM((128, 128), BF16),
                pltpu.VMEM((128, 128), BF16),
                pltpu.VMEM((128, 256), F32),
                pltpu.VMEM((96, 256), BF16),
                pltpu.VMEM((96, 256), BF16),
                tail, tail, tail, tail,
                pltpu.VMEM((8, 256), F32),
                pltpu.VMEM((8, 256), F32),
                pltpu.SemaphoreType.DMA((8,)),
                pltpu.SemaphoreType.DMA((6,)),
                pltpu.SemaphoreType.DMA((6,)),
            ],
            compiler_params=pltpu.CompilerParams(
                collective_id=0, has_side_effects=True, vmem_limit_bytes=32 << 20
            ),
            name="reconstruct",
        )(*[pltpu.with_memory_space_constraint(a, pltpu.HBM) for a in (coarse_scaling, details, two_scale, parent_link)])

    placed = (
        P(None, ("leaf", "sub")),
        P(None, None, ("leaf", "sub")),
        P(),
        P(None, ("leaf", "sub")),
    )
    return jax.shard_map(
        on_device, mesh=mesh, in_specs=placed, out_specs=P(None, ("leaf", "sub")), check_vma=False
    )
```

```python
import jax
import jax.numpy as jnp
from jax import lax
from jax.experimental import pallas as pl
from jax.experimental.pallas import tpu as pltpu
from jax.sharding import PartitionSpec as P

MESH = pl.DeviceIdType.MESH
TAIL = 4
F32, BF16, I32 = jnp.float32, jnp.bfloat16, jnp.int32


def iota(shape, axis):
    return lax.broadcasted_iota(I32, shape, axis)


def nn(a, b):
    return lax.dot_general(a, b, (((1,), (0,)), ((), ())), preferred_element_type=F32)


def nt(a, b):
    return lax.dot_general(a, b, (((1,), (1,)), ((), ())), preferred_element_type=F32)


def split(x):
    hi = x.astype(BF16)
    return hi, (x - hi.astype(F32)).astype(BF16)


def triple(dot, a, b):
    if a[0].shape[1] != 128:
        return dot(a[0], b[0]) + dot(a[1], b[0]) + dot(a[0], b[1])
    doubled = jnp.concatenate([b[0], b[0]], 0 if dot is nn else 1)
    return dot(jnp.concatenate([a[0], a[1]], 1), doubled) + dot(a[0], b[1])


def below(x, rows):
    return jnp.concatenate([x, jnp.zeros((rows, x.shape[1]), x.dtype)], 0)


def flag(mask):
    return jnp.where(mask, 1.0, 0.0)


def one_hot(mask):
    return flag(mask).astype(BF16)


def kernel(
    leafs, subs,
    coarse_hbm, details_hbm, w_hbm, link_hbm, out_ref,
    coarse, details, w_ref, link_ref, x_hi, x_lo, x2, as_hi, as_lo, mixed,
    up_hi, up_lo, quarter, p_hi, p_lo,
    send0, recv0, send1, recv1, send2, recv2, local_sem, send_sem, recv_sem,
):
    leaf, sub = lax.axis_index("leaf"), lax.axis_index("sub")
    device = leaf * subs + sub
    total = leafs * subs
    ahead = lax.rem(device + 1, total)
    behind = lax.rem(device + total - 1, total)
    target = (lax.div(ahead, subs), lax.rem(ahead, subs))
    source = (lax.div(behind, subs), lax.rem(behind, subs))
    has_source, has_target = device > 0, device < total - 1
    patient = sub < 2

    def load(n, src, dst):
        copy = pltpu.make_async_copy(src, dst, local_sem.at[n])
        copy.start()
        return copy

    load_link = load(0, link_hbm, link_ref)
    load_coarse = load(1, coarse_hbm, coarse)
    load_w = load(2, w_hbm, w_ref)
    load_first = []
    for c in range(4):
        rows = pl.ds(128 * c, 128)
        load_first.append(load(4 + c, details_hbm.at[0, :, rows, :], details.at[0, :, rows, :]))
    load_second = load(3, details_hbm.at[1], details.at[1])

    barrier = pltpu.get_barrier_semaphore()

    @pl.when(has_source)
    def _():
        pl.semaphore_signal(barrier, inc=1, device_id=source, device_id_type=MESH)

    def hop(n, src, dst):
        return pltpu.make_async_remote_copy(
            src_ref=src, dst_ref=dst, send_sem=send_sem.at[n], recv_sem=recv_sem.at[n],
            device_id=target, device_id_type=MESH,
        )

    hop0 = [hop(2 + c, send0.at[pl.ds(16 * c, 16), :], recv0.at[pl.ds(16 * c, 16), :]) for c in range(4)]
    hop1, hop2 = hop(0, send1, recv1), hop(1, send2, recv2)

    def fine(row):
        return (((row >> 3) & 1) << 3) + ((row >> 4) << 1) + ((row >> 2) & 1)

    first_child = device * 1024
    slot = iota((1, 128), 1)
    load_link.wait()

    def read_links(level):
        link = link_ref[level : level + 1, :]
        live = link >= 0
        own = link >= first_child
        offset = link - first_child
        parent = jnp.where(own, offset, offset + 8 * TAIL) >> 3
        octant = link & 7
        group = (slot - octant) >> 3
        return live, own, live & (link < first_child), parent, octant, group

    def parents_of(links):
        live, own, before, parent, octant, group = links
        start = own & (octant == 0)
        lead = one_hot(((slot >> 3) == iota((16, 128), 0)) & start)
        match = one_hot(iota((128, 128), 0) == parent)
        return nt(lead, match)

    links1, links2 = read_links(0), read_links(1)
    r16, s16 = iota((16, 128), 0), iota((16, 128), 1)
    tails = flag((r16 < 8) & (s16 == 128 - TAIL + (r16 & 3)))
    chosen1, chosen2 = parents_of(links1), parents_of(links2)
    pick1 = jnp.concatenate([chosen1, tails], 0).astype(BF16)
    pick2 = jnp.concatenate([chosen2, tails], 0).astype(BF16)

    upper = iota((8, 256), 0) < 4

    def stacked(level, a, i):
        first = 64 * i
        return [details[level, 4 * a + q - 1, pl.ds(first, 64), :] for q in range(4) if 4 * a + q]

    load_coarse.wait()
    first_half = iota((32, 128), 1) < 64

    def parents_blocks(c):
        hi, lo = split(coarse[pl.ds(128 * c, 128), :])
        finer = nt(pick1, lo)
        pairs = []
        for n in range(2):
            i = 2 * c + n
            even = nt(pick1, jnp.concatenate([hi[64 * n : 64 * n + 64]] + stacked(0, 0, i), 0))
            rest = jnp.where(first_half, pltpu.roll(finer, 64, 1) if n else finer, 0.0)
            even = jnp.concatenate([even[:, :128] + rest, even[:, 128:]], 1)
            pairs.append((even, nt(pick1, jnp.concatenate(stacked(0, 1, i), 0))))
        return pairs

    def keep_piece(c, pairs):
        for i, (even, odd) in zip((2 * c, 2 * c + 1), pairs):
            e_hi, e_lo = split(even[:16])
            x_hi[pl.ds(16 * i, 16), :] = e_hi
            x_lo[pl.ds(16 * i, 16), :] = e_lo
            x_hi[pl.ds(128 + 16 * i, 16), :] = odd[:16].astype(BF16)

    def send_piece(c, pairs):
        for half in range(2):
            first, second = pairs[0][half], pairs[1][half]
            send0[pl.ds(16 * c + 8 * half, 8), :] = jnp.where(upper, first[16:24], second[16:24])

        @pl.when(has_target & ~patient)
        def _():
            if c == 0:
                pl.semaphore_wait(barrier, 1)
            hop0[c].start()

    pieces = []
    for c in range(4):
        load_first[c].wait()
        pieces.append(parents_blocks(c))
        if c:
            send_piece(c - 1, pieces[c - 1])
    send_piece(3, pieces[3])
    for c in range(4):
        keep_piece(c, pieces[c])

    load_second.wait()
    held = [None, None]
    for i in range(8):
        even = nt(pick2, jnp.concatenate([jnp.zeros((64, 128), BF16)] + stacked(1, 0, i), 0))
        odd = nt(pick2, jnp.concatenate(stacked(1, 1, i), 0))
        x2[pl.ds(16 * i, 16), :] = even[:16].astype(BF16)
        x2[pl.ds(128 + 16 * i, 16), :] = odd[:16].astype(BF16)
        if i % 2:
            send1[pl.ds(8 * i - 8, 8), :] = jnp.where(upper, held[0], even[16:24])
            send1[pl.ds(8 * i, 8), :] = jnp.where(upper, held[1], odd[16:24])
        held = [even[16:24], odd[16:24]]

    @pl.when(has_target & ~patient)
    def _():
        hop1.start()

    load_w.wait()
    w = w_ref[...]
    w_hi, w_lo = split(w)
    row, lane = iota((256, 32), 0), iota((256, 32), 1)
    at_outer = one_hot((lane & 15) == ((row >> 7) << 3) + ((row >> 3) & 7))
    at_inner = one_hot((lane & 15) == (((row >> 6) & 1) << 3) + (row & 7))
    tall = jnp.concatenate([w_hi, w_lo], 0)
    wide = jnp.concatenate([tall, tall], 1)

    def spread(at):
        rows = nn(at, wide)
        top = rows.astype(BF16).astype(F32)
        return nt(jnp.where(lane < 16, top, rows - top).astype(BF16), at)

    kw = split(spread(at_outer) * spread(at_inner))

    live1, own1, before1, parent1, octant1, group1 = links1
    turned = jnp.concatenate([w[8:16], w[0:8]], 0)
    t_hi, t_lo = split(turned)
    x192, c192 = iota((16, 192), 0), iota((16, 192), 1)
    fits = x192 == fine(c192 & 63)
    middle = (c192 >> 6) == 1
    lift = nn(t_hi, one_hot(fits & ~middle)) + nn(t_lo, one_hot(fits & middle))
    lift = jnp.where((c192 & 3) == parent1[:, 127:128], lift, 0.0).astype(BF16)

    live2, own2, before2, parent2, octant2, group2 = links2
    base = tuple(jnp.concatenate([k[:, :64], k[:, :64]], 1) for k in kw)

    def folded(block, quarters):
        parts = [jnp.where(quarters == q, block[64 * q : 64 * q + 64], 0.0) for q in range(4)]
        return (parts[0] + parts[1]) + (parts[2] + parts[3])

    def own_work():
        att = iota((64, 128), 0)
        traits = (
            (own1 & (att == group1))
            | (before1 & (att == 16 + parent1))
            | (live1 & (att == 20 + (octant1 >> 2)))
            | (live1 & (att == 24 + (octant1 & 3)))
        )
        boxes = nt(chosen2.astype(BF16), one_hot(traits)).astype(BF16)
        per_row = nn(one_hot(iota((128, 16), 1) == (iota((128, 16), 0) & 15)), boxes).astype(BF16)
        trait, col = iota((64, 768), 0), iota((64, 768), 1)
        table = (
            ((col < 256) & (trait == (col & 15)))
            | ((col >= 256) & (col < 320) & (trait == 16 + (col & 3)))
            | ((col >= 384) & (col < 640) & (trait == 24 + ((col - 384) >> 6)))
            | ((col >= 640) & (col < 656) & (trait == 20 + ((col - 640) >> 3)))
        )
        masks = nn(per_row, one_hot(table))
        rho, y128 = iota((128, 128), 0), iota((128, 128), 1)
        choose = jnp.where((y128 & 7) == (rho >> 4), masks[:, 640:768], 0.0).astype(BF16)
        x384, c384 = iota((16, 384), 0), iota((16, 384), 1)
        columns = one_hot(x384 == jnp.where(c384 < 256, c384 >> 4, fine(c384 - 256)))
        pad = jnp.zeros((112, 384), BF16)
        keep = masks[:, :384]

        def lifted(part):
            rows = jnp.concatenate([nn(part, columns).astype(BF16), pad], 0)
            return (nn(choose, rows) * keep).astype(BF16)

        raised = lifted(w_hi), lifted(w_lo)
        up_hi[...], up_lo[...] = raised[0][:, 256:], raised[1][:, 256:]
        quarter[...] = masks[:, 384:640]
        own_up = (raised[0][:, :256], raised[1][:, :256])
        y1 = nt(x_hi[...], kw[0]) + nt(x_hi[...], kw[1])
        y1 = y1 + below(nt(x_lo[...], kw[0]), 128)
        v = triple(nn, own_up, split(y1)) * masks[:, 384:640]
        v = v[:, :128] + v[:, 128:]

        at_fine = one_hot(iota((256, 16), 1) == (iota((256, 16), 0) >> 4))
        down = (nt(at_fine, w_hi).astype(BF16), nt(at_fine, w_lo).astype(BF16))
        mine = own2 & ((iota((256, 128), 0) & 15) == group2)
        for i in range(8):
            which = one_hot(live2 & (r16 == ((octant2 >> 2) << 3) + i))
            as_hi[:, pl.ds(128 * i, 128)] = jnp.where(mine, nn(down[0], which), 0.0).astype(BF16)
            as_lo[:, pl.ds(128 * i, 128)] = jnp.where(mine, nn(down[1], which), 0.0).astype(BF16)

        det = nt(kw[0], x2[...]) + nt(kw[1], x2[...])
        own_scaled = triple(nt, base, split(v))
        y2 = split(jnp.concatenate([det[:, :128] + own_scaled, det[:, 128:]], 1))

        for i in range(0, 8, 2):
            lanes = pl.ds(128 * i, 256)
            block = triple(nn, y2, (as_hi[:, lanes], as_lo[:, lanes]))
            for n in range(2):
                out_ref[pl.ds(64 * (i + n), 64), :] = folded(block[:, 128 * n : 128 * n + 128], octant2 & 3)

        names = one_hot(before2 & (parent2 == r16))
        c128 = iota((128, 256), 1)
        named = nn(names, one_hot(iota((128, 256), 0) == 96 + (c128 & 31))).astype(BF16)
        row96, x96 = iota((96, 16), 0), iota((96, 16), 1)
        late = row96 - 64
        comes = nn(one_hot(x96 == jnp.where(row96 < 64, row96 & 3, late >> 3)), named)
        at_prev = one_hot(x96 == jnp.where(row96 < 64, fine(row96 & 63), late & 7))
        c16 = iota((16, 256), 1)
        which = one_hot(iota((16, 256), 0) == (((c16 >> 2) & 1) << 3) + (c16 >> 5))

        def dropped(part):
            return (nn(nt(at_prev, part).astype(BF16), which) * comes).astype(BF16)

        p_hi[...], p_lo[...] = dropped(w_hi), dropped(w_lo)

    def messages():
        @pl.when(has_target & patient)
        def _():
            pl.semaphore_wait(barrier, 1)
            for copy in hop0:
                copy.start()
            hop1.start()

        @pl.when(has_source)
        def _():
            for copy in hop0:
                copy.wait_recv()
            hi, lo = split(recv0[...])
            mixed[...] = nn(lift, jnp.concatenate([hi, hi, lo], 0))[:8]

        @pl.when(device == 0)
        def _():
            recv0[...] = jnp.zeros((64, 256), F32)
            recv1[...] = jnp.zeros((64, 256), F32)
            recv2[...] = jnp.zeros((8, 256), F32)
            x256, c256 = iota((16, 256), 0), iota((16, 256), 1)
            fits = one_hot((x256 == (c256 >> 4)) & ((c256 & 15) == 15))
            l_hi, l_lo = nn(t_hi, fits).astype(BF16), nn(t_lo, fits).astype(BF16)
            both = nn(l_hi, x_hi[...]) + nn(l_lo, x_hi[...]) + nn(l_hi[:, :128], x_lo[...])
            mixed[...] = both[:8]

        @pl.when(has_target)
        def _():
            top = mixed[...].astype(BF16).astype(F32)
            pair = jnp.concatenate([top, mixed[...] - top], 0).astype(BF16)
            main = nt(pair, kw[0])
            send2[...] = main[:8] + main[8:] + nt(pair, kw[1])[:8]
            hop2.start()

    @pl.loop(0, 2)
    def _(n):
        turn = (n == 0) == patient
        pl.when(turn)(own_work)
        pl.when(jnp.logical_not(turn))(messages)

    tail_y = triple(nt, split(recv0[...]), kw)
    v = triple(nn, (up_hi[...], up_lo[...]), split(below(tail_y, 64))) * quarter[...]
    v = v[:, :128] + v[:, 128:]
    scaling = split(triple(nt, base, split(v)))
    for i in range(0, 8, 2):
        lanes = pl.ds(128 * i, 256)
        block = triple(nn, scaling, (as_hi[:128, lanes], as_lo[:128, lanes]))
        for n in range(2):
            out_ref[pl.ds(64 * (i + n), 64), :] += folded(block[:, 128 * n : 128 * n + 128], octant2 & 3)

    top64, low64, top32, low32 = p_hi[:64, :], p_lo[:64, :], p_hi[64:, :], p_lo[64:, :]
    main = jnp.concatenate([top64, top64, below(jnp.concatenate([top32, top32, low32], 0), 32)], 0)
    extra = below(low64, 64)
    static = iota((64, 256), 1) & 3
    reach = (iota((128, 128), 1) >> 6) == ((iota((128, 128), 0) >> 3) & 1)
    third = iota((256, 128), 1) >> 5

    @pl.when(has_source)
    def _():
        hop1.wait_recv()
        tail2 = recv1[...].astype(BF16)
        tail2 = jnp.concatenate([tail2, tail2], 0)
        det2 = nt(kw[0], tail2) + nt(kw[1], tail2)
        det_top = det2.astype(BF16)
        upper_part = det_top.astype(F32)
        det_both = jnp.where(third < 2, upper_part, det2 - upper_part).astype(BF16)
        hop2.wait_recv()
        left, right = recv2[:, :128], recv2[:, 128:]
        parts = split(jnp.where(reach, jnp.concatenate([left, left, right, right] * 4, 0), 0.0))
        last = triple(nt, base, parts)
        top = last.astype(BF16).astype(F32)
        last = jnp.where(third == 1, last - top, top).astype(BF16)
        block = nn(jnp.concatenate([det_both, last], 1), main) + nn(det_top, extra)
        block = folded(block, static)
        for i in range(8):
            tile = block[:, 128 * (i // 4) : 128 * (i // 4) + 128]
            if i % 4 < 3:
                tile = pltpu.roll(tile, 96 - 32 * (i % 4), 1)
            rows = pl.ds(64 * i, 64)
            out_ref[rows, :] = jnp.where(before2, tile, out_ref[rows, :])

    @pl.when(has_target)
    def _():
        for copy in hop0 + [hop1, hop2]:
            copy.wait_send()


def solution(mesh):
    leafs, subs = mesh.shape["leaf"], mesh.shape["sub"]

    def on_device(coarse_scaling, details, two_scale, parent_link):
        outside = pl.BlockSpec(memory_space=pltpu.HBM)
        details = details.reshape(2, 7, 512, 128)
        tail = pltpu.VMEM((64, 256), F32)
        return pl.pallas_call(
            lambda *refs: kernel(leafs, subs, *refs),
            out_shape=jax.ShapeDtypeStruct(coarse_scaling.shape, F32),
            in_specs=[outside] * 4,
            out_specs=pl.BlockSpec(memory_space=pltpu.VMEM),
            scratch_shapes=[
                pltpu.VMEM(coarse_scaling.shape, F32),
                pltpu.VMEM(details.shape, BF16),
                pltpu.VMEM(two_scale.shape, F32),
                pltpu.VMEM(parent_link.shape, I32),
                pltpu.VMEM((256, 256), BF16),
                pltpu.VMEM((128, 256), BF16),
                pltpu.VMEM((256, 256), BF16),
                pltpu.VMEM((256, 1024), BF16),
                pltpu.VMEM((256, 1024), BF16),
                pltpu.VMEM((8, 256), F32),
                pltpu.VMEM((128, 128), BF16),
                pltpu.VMEM((128, 128), BF16),
                pltpu.VMEM((128, 256), F32),
                pltpu.VMEM((96, 256), BF16),
                pltpu.VMEM((96, 256), BF16),
                tail, tail, tail, tail,
                pltpu.VMEM((8, 256), F32),
                pltpu.VMEM((8, 256), F32),
                pltpu.SemaphoreType.DMA((8,)),
                pltpu.SemaphoreType.DMA((6,)),
                pltpu.SemaphoreType.DMA((6,)),
            ],
            compiler_params=pltpu.CompilerParams(
                collective_id=0, has_side_effects=True, vmem_limit_bytes=32 << 20
            ),
            name="reconstruct",
        )(*[pltpu.with_memory_space_constraint(a, pltpu.HBM) for a in (coarse_scaling, details, two_scale, parent_link)])

    placed = (
        P(None, ("leaf", "sub")),
        P(None, None, ("leaf", "sub")),
        P(),
        P(None, ("leaf", "sub")),
    )
    return jax.shard_map(
        on_device, mesh=mesh, in_specs=placed, out_specs=P(None, ("leaf", "sub")), check_vma=False
    )
```
